512 devices in a mesh: sub: 128 (over y, z, core), split: 4 (over x).
Axes of the slice: x: 4, y: 8, z: 8, core: 2. Of those that a mesh axis runs over, the one named last changes fastest.
Arguments:
- inv_conductance: float32 [128, 2048, 2048], P('sub', None, 'split')
- source_amp: float32 [128, 2048], P('sub', 'split'), may hold values from -6 to 6
- source_phase: float32 [128, 2048], P('sub', 'split'), may hold values from -3.140625 to 3.140625
- companion: float32 [128, 2048], P('sub', 'split'), may hold values from 0.1 to 0.8
- surge_impedance: float32 [128, 512], P('sub', 'split'), may hold values from 2 to 8
- initial_voltage: float32 [128, 64, 2048], P('sub', None, 'split'), may hold values from -6 to 6
- initial_history: float32 [128, 64, 512], P('sub', None, 'split'), may hold values from -6 to 6
- partner_sub: int32 [128, 512], P('sub', 'split'), may hold values from 0 to 127, as said below
- line_delay: int32 [128, 512], P('sub', 'split'), may hold values from 2 to 5, as said below
- open_step: int32 [128, 64, 512], P('sub', None, 'split'), may hold values from 0 to 15
Outputs:
- voltage: float32 [128, 64, 2048], P('sub', None, 'split')
- port_current: float32 [128, 64, 512], P('sub', None, 'split')
The draws below stay inside these ranges and needn't reach their ends.
Inputs may be any that keep to these rules, and one draw needn't show every extreme that they name: partner_sub[partner_sub[s, p], p] == s and partner_sub[s, p] != s: a line joins port p of two subnetworks, both in the same block of 128 ports. At most 2 ports of one block of a subnetwork have lines to the same other subnetwork, and in every block some subnetwork gets exactly 2. `line_delay`: both ends of a line have the same delay.
All inputs are finite; a program needn't handle non-finite values.
Results may differ from the reference program's by a relative error of at most 0.00015.
Values sent between devices are 32-bit elements; how exact they have to be, the bound alone decides.
No kernel may reach another device: no remote copies, remote signals or barrier semaphores. Data moves between devices by JAX's collectives and lax.ppermute only.
A program may use at most 64 MiB of HBM per device.

```python
import math
import jax
import jax.numpy as jnp
from jax import lax

NODES = 2048
PORTS = 512
CONT = 64
STEPS = 8
DMIN = 2
DMAX = 5
SUBS = 128
PORTS_DEV = 128
CAP = 2


def draw_inv_conductance(key, part):
    first, second = jax.random.split(jax.random.fold_in(key, 17))
    diagonal = jax.random.uniform(first, (SUBS, NODES), jnp.float32, 0.3, 0.9)
    spread = jax.random.normal(second, (SUBS, NODES, NODES), jnp.float32) * (0.3 / NODES ** 0.5)
    return spread + diagonal[:, :, None] * jnp.eye(NODES, dtype=jnp.float32)[None]


def line_block(block_key):
    keys = jax.random.split(block_key, 5)
    order = jax.random.permutation(keys[0], PORTS_DEV).astype(jnp.int32)
    relabel = jax.random.permutation(keys[1], SUBS).astype(jnp.int32)
    inverse = jnp.argsort(relabel).astype(jnp.int32)
    offset = jax.random.randint(keys[2], (), 0, SUBS - 1)
    group = order // CAP
    flip = 1 + (group + offset) % (SUBS - 1)
    label = relabel[:, None]
    other = jnp.bitwise_xor(label, flip[None, :])
    partner = inverse[other]
    lower = jnp.minimum(label, other)
    delay_table = jax.random.randint(keys[4], (SUBS, PORTS_DEV), DMIN, DMAX + 1)
    delay = delay_table[lower, order[None, :]]
    return (partner.astype(jnp.int32), delay.astype(jnp.int32))


def line_tables(key):
    blocks = [line_block(jax.random.fold_in(key, 1000 + number)) for number in range(PORTS // PORTS_DEV)]
    return tuple((jnp.concatenate([entry[which] for entry in blocks], 1) for which in range(2)))


def draw_partner_sub(key, part):
    return line_tables(key)[0]


def draw_line_delay(key, part):
    return line_tables(key)[1]


def with_ends(drawn, stream_key, low, largest):
    place = [jax.random.randint(jax.random.fold_in(stream_key, axis), (), 0, length) for axis, length in enumerate(drawn.shape)]
    widest = drawn.shape.index(max(drawn.shape))
    next_to = place[:widest] + [(place[widest] + 1) % drawn.shape[widest]] + place[widest + 1:]
    return drawn.at[tuple(place)].set(low).at[tuple(next_to)].set(largest)


def level_of(key, extent, pieces, least, top_value):
    factor_of = 1.0
    for dim, parts in pieces:
        steps = jax.random.uniform(jax.random.fold_in(jax.random.fold_in(key, 6), dim), (parts,), jnp.float32, least / len(pieces), top_value / len(pieces))
        factor_of = factor_of * jnp.repeat(jnp.exp(steps), extent[dim] // parts).reshape((-1,) + (1,) * (len(extent) - 1 - dim))
    return factor_of


def gaussian(rng, shape, scale, bound, shards=(), kind=jnp.bfloat16):
    gain = level_of(rng, shape, shards, -0.22, 0.18) if shards else 1.0
    drawn = jax.random.normal(rng, shape, jnp.float32) * scale * gain
    return jnp.minimum(jnp.maximum(drawn, -bound), bound).astype(kind)


def setup_inputs(seed: int = 0) -> dict:
    streams_of = jax.random.split(jax.random.key(seed), 11)
    inv_conductance = draw_inv_conductance(jax.random.fold_in(streams_of[10], 71), 0)
    source_amp = gaussian(streams_of[1], (SUBS, NODES), 1.0, 6.0, ((0, 128), (1, 4)), jnp.float32)
    source_phase = jnp.clip(jax.random.uniform(streams_of[2], (SUBS, NODES), jnp.float32, -3.140625, 3.140625), -3.140625, 3.140625)
    companion = jnp.clip(jnp.exp(math.log(0.8) - 2.0794415 * jax.random.uniform(streams_of[3], (SUBS, NODES), jnp.float32) ** level_of(streams_of[3], (SUBS, NODES), ((0, 128), (1, 4)), -0.2, 0.2)), 0.1, 0.8)
    surge_impedance = jnp.clip(jnp.exp(math.log(8.0) - 1.3862944 * jax.random.uniform(streams_of[4], (SUBS, PORTS), jnp.float32) ** level_of(streams_of[4], (SUBS, PORTS), ((0, 128), (1, 4)), -0.2, 0.2)), 2.0, 8.0)
    initial_voltage = gaussian(streams_of[5], (SUBS, CONT, NODES), 1.0, 6.0, ((0, 128), (2, 4)), jnp.float32)
    initial_history = gaussian(streams_of[6], (SUBS, CONT, PORTS), 1.0, 6.0, ((0, 128), (2, 4)), jnp.float32)
    partner_sub = draw_partner_sub(jax.random.fold_in(streams_of[10], 71), 0)
    line_delay = draw_line_delay(jax.random.fold_in(streams_of[10], 71), 0)
    open_step = with_ends(jax.random.randint(streams_of[9], (SUBS, CONT, PORTS), 0, 2 * STEPS), jax.random.fold_in(streams_of[9], 1), 0, (2 * STEPS) - 1).astype(jnp.int32)
    return {"inv_conductance": inv_conductance, "source_amp": source_amp, "source_phase": source_phase, "companion": companion, "surge_impedance": surge_impedance, "initial_voltage": initial_voltage, "initial_history": initial_history, "partner_sub": partner_sub, "line_delay": line_delay, "open_step": open_step}


angular = 0.7


def reference(inv_conductance, source_amp, source_phase, companion, surge_impedance, initial_voltage, initial_history, partner_sub, line_delay, open_step):
    subs = inv_conductance.shape[0]
    cont = initial_voltage.shape[1]
    ports = initial_history.shape[2]
    stride = NODES // PORTS
    voltage = initial_voltage
    delays = line_delay[:, None, :]
    index = jnp.broadcast_to(partner_sub[:, None, :], (subs, cont, ports)).astype(jnp.int32)
    arrived = []
    current = jnp.zeros_like(initial_history)
    for step in range(STEPS):
        closed = (step < open_step).astype(jnp.float32)
        history = jnp.where(step < delays, initial_history, jnp.float32(0.0))
        for anchor, outgoing in enumerate(arrived):
            far_end = jnp.take_along_axis(outgoing, index, axis=0)
            history = jnp.where(delays == step - anchor, -far_end, history)
        inject = closed * history
        spread = jnp.concatenate([inject[:, :, :, None], jnp.zeros((subs, cont, ports, stride - 1), jnp.float32)], 3).reshape(subs, cont, NODES)
        source = source_amp * jnp.cos(angular * (step + 1) + source_phase)
        right_side = source[:, None, :] + companion[:, None, :] * voltage - spread
        voltage = jnp.einsum("scm,snm->scn", right_side, inv_conductance, precision=lax.Precision.HIGHEST)
        at_ports = voltage.reshape(subs, cont, ports, stride)[:, :, :, 0]
        impedance = surge_impedance[:, None, :]
        arrived.append(closed * (2.0 * at_ports / impedance + history))
        current = closed * (at_ports / impedance + history)
    return voltage, current
```

```python
import jax
import jax.numpy as jnp
from jax import lax
from jax.experimental import pallas as pl
from jax.experimental.pallas import tpu as pltpu
from jax.sharding import PartitionSpec as P

STEPS = 8
DMIN = 2
DMAX = 5
STRIDE = 4
PARTS = 4

angular = 0.7

F32 = jnp.float32
BF16 = jnp.bfloat16
NT = (((1,), (1,)), ((), ()))
NN = (((1,), (0,)), ((), ()))
TN = (((0,), (0,)), ((), ()))


def two_pieces(array):
    high = array.astype(BF16)
    return high, (array - high.astype(F32)).astype(BF16)


def exact_dot(array, onehot, dims, array_first=True):
    high = array.astype(BF16)
    rest = array - high.astype(F32)
    middle = rest.astype(BF16)
    low = (rest - middle.astype(F32)).astype(BF16)
    total = None
    for piece in (high, middle, low):
        pair = (piece, onehot) if array_first else (onehot, piece)
        term = lax.dot_general(*pair, dims, preferred_element_type=F32)
        total = term if total is None else total + term
    return total


def iota(shape, dim):
    return lax.broadcasted_iota(jnp.int32, shape, dim)


def first_body(matrix, amp, phase, comp, volt, hist, delay, opens, out, table, stacked):
    cont, nodes = volt.shape
    ports = nodes // STRIDE

    @pl.when(pl.program_id(0) == 0)
    def _():
        times = (iota((STEPS, nodes), 0) + 1).astype(F32)
        source = amp[...] * jnp.cos(angular * times + phase[...])
        table[0:STEPS] = source
        table[STEPS:] = jnp.broadcast_to(comp[...], (STEPS, nodes))
        start = jnp.where(0 < delay[...], hist[...], 0.0)
        inject = jnp.where(0 < opens[...], start, 0.0)
        place = (iota((ports, nodes), 1) == STRIDE * iota((ports, nodes), 0)).astype(F32).astype(BF16)
        right = source[0:1] + comp[...] * volt[...] - exact_dot(inject, place, NN)
        high, low = two_pieces(right)
        stacked[:cont] = high
        stacked[cont:] = low

    high, low = two_pieces(matrix[...])
    both = lax.dot_general(stacked[...], high, NT, preferred_element_type=F32)
    rest = lax.dot_general(stacked[:cont], low, NT, preferred_element_type=F32)
    out[0] = both[:cont] + both[cont:] + rest


def prepare_body(matrix, table, order, high_out, low_out, table_out):
    nodes = matrix.shape[1]
    ports = nodes // STRIDE
    new = iota((nodes, nodes), 0)
    old = STRIDE * (new % ports) + new // ports
    moved = (iota((nodes, nodes), 1) == old).astype(F32).astype(BF16)
    order[...] = moved
    table_out[...] = exact_dot(table[...], moved, NT)
    for part in range(PARTS):
        pieces = two_pieces(matrix[part * nodes : (part + 1) * nodes])
        for piece, piece_out in zip(pieces, (high_out, low_out)):
            inputs = lax.dot_general(moved, piece, NT, preferred_element_type=F32).astype(BF16)
            piece_out[part] = lax.dot_general(inputs, moved, NT, preferred_element_type=F32).astype(BF16)


def history_at(step, start, delay, far):
    history = jnp.where(step < delay, start, 0.0)
    for anchor, array in far:
        history = jnp.where(delay == step - anchor, -array, history)
    return history


def step_body(step, anchors, high, low, table, volt, start, delay, opens, *refs):
    far = [(anchor, ref[...]) for anchor, ref in zip(anchors, refs)]
    out, kept = refs[len(anchors) :]
    cont, nodes = volt.shape
    ports = nodes // STRIDE
    history = history_at(step, start[...], delay[...], far)
    kept[...] = history
    right = table[step : step + 1] + table[STEPS : STEPS + 1] * volt[...]
    inject = jnp.where(step < opens[...], history, 0.0)
    right = jnp.concatenate([right[:, :ports] - inject, right[:, ports:]], 1)
    right_high, right_low = two_pieces(right)
    stacked = jnp.concatenate([right_high, right_low], 0)
    for part in range(PARTS):
        both = jnp.dot(stacked, high[part], preferred_element_type=F32)
        rest = jnp.dot(right_high, low[part], preferred_element_type=F32)
        out[part] = both[:cont] + both[cont:] + rest


def total_of(partial):
    total = partial[0]
    for part in range(1, PARTS):
        total = total + partial[part]
    return total


def close_body(step, partial, impedance, history, opens, *refs):
    volt, outgoing = refs[-2:]
    total = total_of(partial)
    if step == 0:
        total = exact_dot(total, refs[0][...], NT)
    volt[...] = total
    ports = impedance.shape[1]
    value = 2.0 * total[:, :ports] / impedance[...] + history[...]
    outgoing[...] = jnp.where(step < opens[...], value, 0.0)


def route_body(step, partial, impedance, history, opens, target, before, volt, buffer):
    total = total_of(partial)
    volt[...] = total
    slots = buffer.shape[0]
    ports = impedance.shape[1]
    value = 2.0 * total[:, :ports] / impedance[...] + history[...]
    outgoing = jnp.where(step < opens[...], value, 0.0)
    both = jnp.concatenate([before[...], outgoing], 0)
    routing = (iota((slots, ports), 0) == target[...]).astype(F32).astype(BF16)
    buffer[...] = exact_dot(both, routing, NT, array_first=False)


def unroute_body(buffer, target, first, second):
    slots = buffer.shape[0]
    cont, ports = first.shape
    routing = (iota((slots, ports), 0) == target[...]).astype(F32).astype(BF16)
    both = exact_dot(buffer[...], routing, TN)
    first[...] = both[:cont]
    second[...] = both[cont:]


def last_body(step, partial, impedance, history, opens, order, volt, current):
    total = total_of(partial)
    ports = impedance.shape[1]
    value = total[:, :ports] / impedance[...] + history[...]
    current[...] = jnp.where(step < opens[...], value, 0.0)
    volt[...] = exact_dot(total, order[...], NN)


def call(body, shapes, *arrays, name):
    whole = pl.BlockSpec(memory_space=pltpu.VMEM)
    return pl.pallas_call(
        body,
        in_specs=[whole] * len(arrays),
        out_specs=[whole] * len(shapes),
        out_shape=[jax.ShapeDtypeStruct(shape, kind) for shape, kind in shapes],
        compiler_params=pltpu.CompilerParams(vmem_limit_bytes=40 << 20),
        name=name,
    )(*arrays)


def local(
    inv_conductance,
    source_amp,
    source_phase,
    companion,
    surge_impedance,
    initial_voltage,
    initial_history,
    partner_sub,
    line_delay,
    open_step,
):
    matrix = inv_conductance[0]
    n_subs = lax.axis_size("sub")
    cont, nodes = initial_voltage.shape[1:]
    ports = initial_history.shape[2]
    capacity = max(2, 2 * ports // n_subs)
    slots = n_subs * capacity
    start = initial_history[0]
    opens = open_step[0]
    delay = line_delay
    impedance = surge_impedance

    small = lambda shape: pl.BlockSpec(shape, lambda part: (0, 0))
    partial, table = pl.pallas_call(
        first_body,
        grid=(PARTS,),
        in_specs=[
            pl.BlockSpec((nodes, nodes), lambda part: (part, 0)),
            small((1, nodes)),
            small((1, nodes)),
            small((1, nodes)),
            small((cont, nodes)),
            small((cont, ports)),
            small((1, ports)),
            small((cont, ports)),
        ],
        out_specs=[
            pl.BlockSpec((1, cont, nodes), lambda part: (part, 0, 0)),
            small((2 * STEPS, nodes)),
        ],
        out_shape=[
            jax.ShapeDtypeStruct((PARTS, cont, nodes), F32),
            jax.ShapeDtypeStruct((2 * STEPS, nodes), F32),
        ],
        scratch_shapes=[pltpu.VMEM((2 * cont, nodes), BF16)],
        name="first_step",
    )(matrix, source_amp, source_phase, companion, initial_voltage[0], start, delay, opens)

    order, high, low, table = call(
        prepare_body,
        [
            ((nodes, nodes), BF16),
            ((PARTS, nodes, nodes), BF16),
            ((PARTS, nodes, nodes), BF16),
            ((2 * STEPS, nodes), F32),
        ],
        matrix,
        table,
        name="prepare",
    )
    partner = partner_sub[0]
    position = jnp.arange(ports, dtype=jnp.int32)
    same_far = partner[:, None] == partner[None, :]
    earlier = position[:, None] > position[None, :]
    slot_rank = jnp.sum((same_far & earlier).astype(jnp.int32), axis=1)
    target = (partner * capacity + slot_rank)[None, :]

    history = start
    far = []
    before = None
    for step in range(STEPS):
        if step > 0:
            anchors = [a for a in range(len(far)) if DMIN <= step - a <= DMAX]
            partial, history = call(
                lambda *refs, step=step, anchors=anchors: step_body(step, anchors, *refs),
                [((PARTS, cont, nodes), F32), ((cont, ports), F32)],
                high,
                low,
                table,
                volt,
                start,
                delay,
                opens,
                *[far[a] for a in anchors],
                name=f"step_{step}",
            )
        arrived = lax.all_to_all(partial, "split", split_axis=0, concat_axis=0, tiled=True)
        if step == STEPS - 1:
            volt, current = call(
                lambda *refs, step=step: last_body(step, *refs),
                [((cont, nodes), F32), ((cont, ports), F32)],
                arrived,
                impedance,
                history,
                opens,
                order,
                name="last",
            )
        elif step + DMIN < STEPS and step % 2 == 1:
            volt, buffer = call(
                lambda *refs, step=step: route_body(step, *refs),
                [((cont, nodes), F32), ((slots, 2 * cont), F32)],
                arrived,
                impedance,
                history,
                opens,
                target,
                before,
                name=f"route_{step}",
            )
            buffer = buffer.reshape(n_subs, capacity, 2 * cont)
            incoming = lax.all_to_all(buffer, "sub", split_axis=0, concat_axis=0, tiled=True)
            far += call(
                unroute_body,
                [((cont, ports), F32), ((cont, ports), F32)],
                incoming.reshape(slots, 2 * cont),
                target,
                name=f"unroute_{step}",
            )
        else:
            volt, before = call(
                lambda *refs, step=step: close_body(step, *refs),
                [((cont, nodes), F32), ((cont, ports), F32)],
                arrived,
                impedance,
                history,
                opens,
                *([order] if step == 0 else []),
                name=f"close_{step}",
            )
    return (volt[None], current[None])


def solution(mesh):
    placed = (
        P("sub", None, "split"),
        P("sub", "split"),
        P("sub", "split"),
        P("sub", "split"),
        P("sub", "split"),
        P("sub", None, "split"),
        P("sub", None, "split"),
        P("sub", "split"),
        P("sub", "split"),
        P("sub", None, "split"),
    )
    return jax.shard_map(
        local,
        mesh=mesh,
        in_specs=placed,
        out_specs=(P("sub", None, "split"), P("sub", None, "split")),
        check_vma=False,
    )
```

```python
import jax
import jax.numpy as jnp
from jax import lax
from jax.experimental import pallas as pl
from jax.experimental.pallas import tpu as pltpu
from jax.sharding import PartitionSpec as P

STEPS = 8
DMIN = 2
DMAX = 5
STRIDE = 4
PARTS = 4
NEAR = 1

angular = 0.7

F32 = jnp.float32
BF16 = jnp.bfloat16
NT = (((1,), (1,)), ((), ()))
NN = (((1,), (0,)), ((), ()))
TN = (((0,), (0,)), ((), ()))


def two_pieces(array):
    high = array.astype(BF16)
    return high, (array - high.astype(F32)).astype(BF16)


def exact_dot(array, onehot, dims, array_first=True):
    high = array.astype(BF16)
    rest = array - high.astype(F32)
    middle = rest.astype(BF16)
    low = (rest - middle.astype(F32)).astype(BF16)
    total = None
    for piece in (high, middle, low):
        pair = (piece, onehot) if array_first else (onehot, piece)
        term = lax.dot_general(*pair, dims, preferred_element_type=F32)
        total = term if total is None else total + term
    return total


def stacked_exact_dot(array, onehot, dims):
    rows = array.shape[0]
    high = array.astype(BF16)
    rest = array - high.astype(F32)
    middle = rest.astype(BF16)
    low = (rest - middle.astype(F32)).astype(BF16)
    pieces = jnp.concatenate([high, middle, low], 0)
    terms = lax.dot_general(pieces, onehot, dims, preferred_element_type=F32)
    return terms[:rows] + terms[rows : 2 * rows] + terms[2 * rows :]


def iota(shape, dim):
    return lax.broadcasted_iota(jnp.int32, shape, dim)


def start_strips(matrix, strips, sems, forward=True):
    copies = {}
    width = strips.shape[2]
    for part in range(PARTS) if forward else reversed(range(PARTS)):
        rows = pl.ds(part * strips.shape[1] // PARTS, strips.shape[1] // PARTS)
        for strip in range(strips.shape[0]):
            copies[part, strip] = pltpu.make_async_copy(
                matrix.at[rows, pl.ds(strip * width, width)],
                strips.at[strip, rows, :],
                sems.at[part, strip],
            )
            copies[part, strip].start()
    return copies


def part_rows(strips, copies, part):
    count, rows, width = strips.shape
    nodes = rows // PARTS
    ports = nodes // STRIDE
    columns = []
    for strip in range(count):
        copies[part, strip].wait()
        pieces = [
            strips[strip, pl.ds(part * nodes + lane, ports, stride=STRIDE), :] for lane in range(STRIDE)
        ]
        columns.append(jnp.concatenate(pieces, 0))
    return jnp.concatenate(columns, 1)


def product(stacked, cont, high, low, dims):
    both = lax.dot_general(stacked, high, dims, preferred_element_type=F32)
    rest = lax.dot_general(stacked[:cont], low, dims, preferred_element_type=F32)
    return both[:cont] + both[cont:] + rest


def first_body(*refs):
    ins, (matrix, table, out, *held, small_sems, strips, sems, block, sent) = refs[:7], refs[7:]
    fetches = [pltpu.make_async_copy(a, b, small_sems.at[n]) for n, (a, b) in enumerate(zip(ins, held))]
    for copy in fetches:
        copy.start()
    copies = start_strips(matrix, strips, sems)
    for copy in fetches:
        copy.wait()
    amp, phase, comp, volt, start, delay, opens = held
    cont, nodes = volt.shape
    ports = nodes // STRIDE
    times = (iota((STEPS, nodes), 0) + 1).astype(F32)
    source = amp[...] * jnp.cos(angular * times + phase[...])
    table[0:STEPS] = source
    table[STEPS:] = jnp.broadcast_to(comp[...], (STEPS, nodes))
    history = jnp.where(0 < delay[...], start[...], 0.0)
    inject = jnp.where(0 < opens[...], history, 0.0)
    place = (iota((ports, nodes), 1) == STRIDE * iota((ports, nodes), 0)).astype(F32).astype(BF16)
    right = source[0:1] + comp[...] * volt[...] - stacked_exact_dot(inject, place, NN)
    stacked = jnp.concatenate(two_pieces(right), 0)
    leaving = []
    for part in range(PARTS):
        high, low = two_pieces(part_rows(strips, copies, part))
        block[part] = product(stacked, cont, high, low, NT)
        leaving.append(pltpu.make_async_copy(block.at[part], out.at[part], sent.at[part]))
        leaving[-1].start()
    for copy in leaving:
        copy.wait()


def prepare_body(
    capacity, table, partner, matrix, low_out, high_near, table_out, target, order_out, high_far, strips, sems, high, order, sent
):
    copies = start_strips(matrix, strips, sems, forward=False)
    nodes = table.shape[1]
    ports = nodes // STRIDE
    new = iota((nodes, nodes), 0)
    old = STRIDE * (new % ports) + new // ports
    moved = (iota((nodes, nodes), 1) == old).astype(F32).astype(BF16)
    order[...] = moved
    leaving = [pltpu.make_async_copy(order, order_out, sent.at[PARTS - NEAR])]
    leaving[-1].start()
    table_out[...] = stacked_exact_dot(table[...], moved, NT)
    across = jnp.broadcast_to(partner[...].astype(F32), (ports, ports))
    earlier = (across == across.T) & (iota((ports, ports), 0) < iota((ports, ports), 1))
    rank = jnp.sum(earlier.astype(F32), axis=0, keepdims=True).astype(jnp.int32)
    target[...] = partner[...] * capacity + rank
    for part in reversed(range(PARTS)):
        pieces = two_pieces(part_rows(strips, copies, part))
        terms = [lax.dot_general(moved, piece, NT, preferred_element_type=F32).astype(BF16) for piece in pieces]
        low_out[part] = terms[1]
        if part < NEAR:
            high_near[part] = terms[0]
        else:
            far = part - NEAR
            high[far] = terms[0]
            leaving.append(pltpu.make_async_copy(high.at[far], high_far.at[far], sent.at[far]))
            leaving[-1].start()
    for copy in leaving:
        copy.wait()


def history_at(step, start, delay, far):
    history = jnp.where(step < delay, start, 0.0)
    for anchor, array in far:
        history = jnp.where(delay == step - anchor, -array, history)
    return history


def total_of(partial):
    total = partial[0]
    for part in range(1, PARTS):
        total = total + partial[part]
    return total


def outgoing_of(step, total, impedance, history, opens):
    ports = impedance.shape[1]
    value = 2.0 * total[:, :ports] / impedance[...] + history
    return jnp.where(step < opens[...], value, 0.0)


def onehot_of(target, slots):
    return (iota((slots, target.shape[1]), 0) == target[...]).astype(F32).astype(BF16)


def multiply(step, volt, history, highs, low, table, opens, out):
    cont, nodes = volt.shape
    ports = nodes // STRIDE
    right = table[step : step + 1] + table[STEPS : STEPS + 1] * volt
    inject = jnp.where(step < opens[...], history, 0.0)
    right = jnp.concatenate([right[:, :ports] - inject, right[:, ports:]], 1)
    stacked = jnp.concatenate(two_pieces(right), 0)
    for part in range(PARTS):
        high = highs[0][part] if part < NEAR else highs[1][part - NEAR]
        out[part] = product(stacked, cont, high, low[part], NN)


def odd_body(step, anchors, near, high, low, table, start, delay, opens, impedance, history, partial, *refs):
    far = [(anchor, ref[...]) for anchor, ref in zip(anchors, refs)]
    out, kept, *outgoing = refs[len(anchors) :]
    total = total_of(partial)
    for ref in outgoing:
        ref[...] = outgoing_of(step - 1, total, impedance, history[...], opens)
    now = history_at(step, start[...], delay[...], far)
    kept[...] = now
    multiply(step, total, now, (near, high), low, table, opens, out)


def even_body(step, anchors, near, high, low, table, start, delay, opens, target, volt, buffer, *refs):
    out, kept, *newest = refs[len(anchors) :]
    cont, ports = start.shape
    both = exact_dot(buffer[...], onehot_of(target, buffer.shape[0]), TN)
    latest = [both[:cont], both[cont:]]
    for ref, array in zip(newest, latest):
        ref[...] = array
    far = [(anchor, ref[...]) for anchor, ref in zip(anchors, refs)] + [(step - DMIN, latest[0])]
    now = history_at(step, start[...], delay[...], far)
    kept[...] = now
    multiply(step, volt[...], now, (near, high), low, table, opens, out)


def route_body(step, partial, impedance, history, opens, target, before, volt, buffer):
    total = total_of(partial)
    volt[...] = total
    outgoing = outgoing_of(step, total, impedance, history[...], opens)
    both = jnp.concatenate([before[...], outgoing], 0)
    buffer[...] = exact_dot(both, onehot_of(target, buffer.shape[0]), NT, array_first=False)


def last_body(step, partial, impedance, history, opens, order, volt, current):
    total = total_of(partial)
    ports = impedance.shape[1]
    value = total[:, :ports] / impedance[...] + history[...]
    current[...] = jnp.where(step < opens[...], value, 0.0)
    volt[...] = stacked_exact_dot(total, order[...], NN)


def call(body, shapes, *arrays, name, far_in=(), far_out=(), scratch=()):
    whole = pl.BlockSpec(memory_space=pltpu.VMEM)
    away = pl.BlockSpec(memory_space=pltpu.HBM)
    return pl.pallas_call(
        body,
        in_specs=[whole] * len(arrays) + [away] * len(far_in),
        out_specs=[whole] * len(shapes) + [away] * len(far_out),
        out_shape=[jax.ShapeDtypeStruct(*shape) for shape in shapes] + [pltpu.HBM(*shape) for shape in far_out],
        scratch_shapes=list(scratch),
        compiler_params=pltpu.CompilerParams(vmem_limit_bytes=40 << 20),
        name=name,
    )(*arrays, *[pltpu.with_memory_space_constraint(array, pltpu.HBM) for array in far_in])


def local(
    inv_conductance,
    source_amp,
    source_phase,
    companion,
    surge_impedance,
    initial_voltage,
    initial_history,
    partner_sub,
    line_delay,
    open_step,
):
    matrix = inv_conductance[0]
    n_subs = lax.axis_size("sub")
    cont, nodes = initial_voltage.shape[1:]
    ports = initial_history.shape[2]
    capacity = max(2, 2 * ports // n_subs)
    slots = n_subs * capacity
    start = initial_history[0]
    opens = open_step[0]
    delay = line_delay
    impedance = surge_impedance
    port_shape = ((cont, ports), F32)
    split_shape = ((PARTS, cont, nodes), F32)

    order_shape = ((nodes, nodes), BF16)
    far_matrix = ((PARTS - NEAR, nodes, nodes), BF16)
    strips = [pltpu.VMEM((STRIDE, PARTS * nodes, ports), F32), pltpu.SemaphoreType.DMA((PARTS, STRIDE))]

    inputs = [source_amp, source_phase, companion, initial_voltage[0], start, delay, opens]
    table, partial = call(
        first_body,
        [((2 * STEPS, nodes), F32)],
        far_in=[*inputs, matrix],
        far_out=[split_shape],
        scratch=[
            *[pltpu.VMEM(array.shape, array.dtype) for array in inputs],
            pltpu.SemaphoreType.DMA((len(inputs),)),
            *strips,
            pltpu.VMEM(*split_shape),
            pltpu.SemaphoreType.DMA((PARTS,)),
        ],
        name="first_step",
    )
    low, near, table, target, order, high = call(
        lambda *refs: prepare_body(capacity, *refs),
        [
            ((PARTS, nodes, nodes), BF16),
            ((NEAR, nodes, nodes), BF16),
            ((2 * STEPS, nodes), F32),
            ((1, ports), jnp.int32),
        ],
        table,
        partner_sub,
        far_in=[matrix],
        far_out=[order_shape, far_matrix],
        scratch=[*strips, pltpu.VMEM(*far_matrix), pltpu.VMEM(*order_shape), pltpu.SemaphoreType.DMA((PARTS - NEAR + 1,))],
        name="prepare",
    )

    history = start
    far = []
    for step in range(STEPS):
        anchors = [a for a in range(step) if DMIN <= step - a <= DMAX]
        if step % 2 == 1:
            partial, history, *before = call(
                lambda *refs, step=step, anchors=anchors: odd_body(step, anchors, *refs),
                [split_shape, port_shape] + [port_shape] * (step + DMIN < STEPS),
                near,
                high,
                low,
                table,
                start,
                delay,
                opens,
                impedance,
                history,
                arrived,
                *[far[a] for a in anchors],
                name=f"step_{step}",
            )
        elif step > 0:
            anchors = anchors[:-1]
            partial, history, *newest = call(
                lambda *refs, step=step, anchors=anchors: even_body(step, anchors, *refs),
                [split_shape] + [port_shape] * 3,
                near,
                high,
                low,
                table,
                start,
                delay,
                opens,
                target,
                volt,
                incoming.reshape(slots, 2 * cont),
                *[far[a] for a in anchors],
                name=f"step_{step}",
            )
            far += newest
        arrived = lax.all_to_all(partial, "split", split_axis=0, concat_axis=0, tiled=True)
        if step == STEPS - 1:
            volt, current = call(
                lambda *refs, step=step: last_body(step, *refs),
                [((cont, nodes), F32), port_shape],
                arrived,
                impedance,
                history,
                opens,
                order,
                name="last",
            )
        elif step % 2 == 1:
            volt, buffer = call(
                lambda *refs, step=step: route_body(step, *refs),
                [((cont, nodes), F32), ((slots, 2 * cont), F32)],
                arrived,
                impedance,
                history,
                opens,
                target,
                *before,
                name=f"route_{step}",
            )
            buffer = buffer.reshape(n_subs, capacity, 2 * cont)
            incoming = lax.all_to_all(buffer, "sub", split_axis=0, concat_axis=0, tiled=True)
    return (volt[None], current[None])


def solution(mesh):
    placed = (
        P("sub", None, "split"),
        P("sub", "split"),
        P("sub", "split"),
        P("sub", "split"),
        P("sub", "split"),
        P("sub", None, "split"),
        P("sub", None, "split"),
        P("sub", "split"),
        P("sub", "split"),
        P("sub", None, "split"),
    )
    return jax.shard_map(
        local,
        mesh=mesh,
        in_specs=placed,
        out_specs=(P("sub", None, "split"), P("sub", None, "split")),
        check_vma=False,
    )
```

```python
import jax
import jax.numpy as jnp
from jax import lax
from jax.experimental import pallas as pl
from jax.experimental.pallas import tpu as pltpu
from jax.sharding import PartitionSpec as P

STEPS = 8
DMIN = 2
DMAX = 5
STRIDE = 4
PARTS = 4

angular = 0.7

F32 = jnp.float32
BF16 = jnp.bfloat16
NT = (((1,), (1,)), ((), ()))
NN = (((1,), (0,)), ((), ()))
TN = (((0,), (0,)), ((), ()))


def two_pieces(array):
    high = array.astype(BF16)
    return high, (array - high.astype(F32)).astype(BF16)


def exact_dot(array, onehot, dims, array_first=True):
    high = array.astype(BF16)
    rest = array - high.astype(F32)
    middle = rest.astype(BF16)
    low = (rest - middle.astype(F32)).astype(BF16)
    total = None
    for piece in (high, middle, low):
        pair = (piece, onehot) if array_first else (onehot, piece)
        term = lax.dot_general(*pair, dims, preferred_element_type=F32)
        total = term if total is None else total + term
    return total


def stacked_exact_dot(array, onehot, dims):
    rows = array.shape[0]
    high = array.astype(BF16)
    rest = array - high.astype(F32)
    middle = rest.astype(BF16)
    low = (rest - middle.astype(F32)).astype(BF16)
    pieces = jnp.concatenate([high, middle, low], 0)
    terms = lax.dot_general(pieces, onehot, dims, preferred_element_type=F32)
    return terms[:rows] + terms[rows : 2 * rows] + terms[2 * rows :]


def iota(shape, dim):
    return lax.broadcasted_iota(jnp.int32, shape, dim)


def start_strips(matrix, strips, sems):
    copies = {}
    width = strips.shape[2]
    for part in range(PARTS):
        rows = pl.ds(part * strips.shape[1] // PARTS, strips.shape[1] // PARTS)
        for strip in range(strips.shape[0]):
            copies[part, strip] = pltpu.make_async_copy(
                matrix.at[rows, pl.ds(strip * width, width)],
                strips.at[strip, rows, :],
                sems.at[part, strip],
            )
            copies[part, strip].start()
    return copies


def strip_rows(strips, part, strip):
    nodes = strips.shape[1] // PARTS
    ports = nodes // STRIDE
    pieces = [strips[strip, pl.ds(part * nodes + lane, ports, stride=STRIDE), :] for lane in range(STRIDE)]
    return jnp.concatenate(pieces, 0)


def port_first(size):
    node = iota((1, size), 1)
    new = (node % STRIDE) * (size // STRIDE) + node // STRIDE
    return (iota((size, size), 0) == new).astype(F32).astype(BF16)


def product(stacked, cont, high, low, dims):
    both = lax.dot_general(stacked, high, dims, preferred_element_type=F32)
    rest = lax.dot_general(stacked[:cont], low, dims, preferred_element_type=F32)
    return both[:cont] + both[cont:] + rest


def first_body(capacity, count, *refs):
    ins, refs = refs[: count + 1], refs[count + 1 :]
    matrix = ins[-1]
    table, target, order, high, low, out, *held = refs
    *held, small_sems, strips, sems = held
    fetches = [pltpu.make_async_copy(a, b, small_sems.at[n]) for n, (a, b) in enumerate(zip(ins, held))]
    for copy in fetches:
        copy.start()
    copies = start_strips(matrix, strips, sems)
    cont, nodes = held[3].shape
    ports = nodes // STRIDE
    moved = port_first(nodes)
    order[...] = moved
    width = 2 * ports
    moved = port_first(width)
    chunk = width // STRIDE
    for copy in fetches:
        copy.wait()
    amp, phase, comp, volt, start, delay, opens, partner = held
    times = (iota((STEPS, nodes), 0) + 1).astype(F32)
    source = amp[...] * jnp.cos(angular * times + phase[...])
    given = jnp.concatenate([volt[...], source, jnp.broadcast_to(comp[...], (STEPS, nodes))], 0)
    given = stacked_exact_dot(given, order[...], NT)
    table[...] = given[cont:]
    across = jnp.broadcast_to(partner[...].astype(F32), (ports, ports))
    earlier = (across == across.T) & (iota((ports, ports), 0) < iota((ports, ports), 1))
    rank = jnp.sum(earlier.astype(F32), axis=0, keepdims=True).astype(jnp.int32)
    target[...] = partner[...] * capacity + rank
    history = history_at(0, start[...], delay[...], [])
    stacked = stacked_right(0, given[:cont], history, table, opens)
    for copy in copies.values():
        copy.wait()
    for part in range(PARTS):
        for pair in range(nodes // width):
            rows = jnp.concatenate([strip_rows(strips, part, strip) for strip in (2 * pair, 2 * pair + 1)], 1)
            for piece, piece_out in zip(two_pieces(rows), (high, low)):
                term = lax.dot_general(moved, piece, NT, preferred_element_type=F32).astype(BF16)
                for lane in range(STRIDE):
                    here = lane * ports + pair * chunk
                    piece_out[part, here : here + chunk, :] = term[lane * chunk : (lane + 1) * chunk]
        if part > 0:
            out[part - 1] = product(stacked, cont, high[part - 1], low[part - 1], NN)
    out[PARTS - 1] = product(stacked, cont, high[PARTS - 1], low[PARTS - 1], NN)


def history_at(step, start, delay, far):
    history = jnp.where(step < delay, start, 0.0)
    for anchor, array in far:
        history = jnp.where(delay == step - anchor, -array, history)
    return history


def total_of(partial):
    total = partial[0]
    for part in range(1, PARTS):
        total = total + partial[part]
    return total


def outgoing_of(step, total, impedance, history, opens):
    ports = impedance.shape[1]
    value = 2.0 * total[:, :ports] / impedance[...] + history
    return jnp.where(step < opens[...], value, 0.0)


def onehot_of(target, slots):
    return (iota((slots, target.shape[1]), 0) == target[...]).astype(F32).astype(BF16)


def stacked_right(step, volt, history, table, opens):
    ports = history.shape[1]
    right = table[step : step + 1] + table[STEPS : STEPS + 1] * volt
    inject = jnp.where(step < opens[...], history, 0.0)
    right = jnp.concatenate([right[:, :ports] - inject, right[:, ports:]], 1)
    return jnp.concatenate(two_pieces(right), 0)


def multiply(step, volt, history, high, low, table, opens, out):
    stacked = stacked_right(step, volt, history, table, opens)
    for part in range(PARTS):
        out[part] = product(stacked, volt.shape[0], high[part], low[part], NN)


def odd_body(step, anchors, high, low, table, start, delay, opens, impedance, history, partial, *refs):
    far = [(anchor, ref[...]) for anchor, ref in zip(anchors, refs)]
    out, kept, *outgoing = refs[len(anchors) :]
    total = total_of(partial)
    for ref in outgoing:
        ref[...] = outgoing_of(step - 1, total, impedance, history[...], opens)
    now = history_at(step, start[...], delay[...], far)
    kept[...] = now
    multiply(step, total, now, high, low, table, opens, out)


def even_body(step, anchors, high, low, table, start, delay, opens, target, volt, buffer, *refs):
    out, kept, *newest = refs[len(anchors) :]
    cont, ports = start.shape
    both = exact_dot(buffer[...], onehot_of(target, buffer.shape[0]), TN)
    latest = [both[:cont], both[cont:]]
    for ref, array in zip(newest, latest):
        ref[...] = array
    far = [(anchor, ref[...]) for anchor, ref in zip(anchors, refs)] + [(step - DMIN, latest[0])]
    now = history_at(step, start[...], delay[...], far)
    kept[...] = now
    multiply(step, volt[...], now, high, low, table, opens, out)


def route_body(step, partial, impedance, history, opens, target, before, volt, buffer):
    total = total_of(partial)
    volt[...] = total
    outgoing = outgoing_of(step, total, impedance, history[...], opens)
    both = jnp.concatenate([before[...], outgoing], 0)
    buffer[...] = exact_dot(both, onehot_of(target, buffer.shape[0]), NT, array_first=False)


def last_body(step, partial, impedance, history, opens, order, volt, current):
    total = total_of(partial)
    ports = impedance.shape[1]
    value = total[:, :ports] / impedance[...] + history[...]
    current[...] = jnp.where(step < opens[...], value, 0.0)
    volt[...] = stacked_exact_dot(total, order[...], NN)


def call(body, shapes, *arrays, name, away=(), scratch=()):
    whole = pl.BlockSpec(memory_space=pltpu.VMEM)
    return pl.pallas_call(
        body,
        in_specs=[whole] * len(arrays) + [pl.BlockSpec(memory_space=pltpu.HBM)] * len(away),
        out_specs=[whole] * len(shapes),
        out_shape=[jax.ShapeDtypeStruct(shape, kind) for shape, kind in shapes],
        scratch_shapes=list(scratch),
        compiler_params=pltpu.CompilerParams(vmem_limit_bytes=40 << 20),
        name=name,
    )(*arrays, *[pltpu.with_memory_space_constraint(array, pltpu.HBM) for array in away])


def local(
    inv_conductance,
    source_amp,
    source_phase,
    companion,
    surge_impedance,
    initial_voltage,
    initial_history,
    partner_sub,
    line_delay,
    open_step,
):
    matrix = inv_conductance[0]
    n_subs = lax.axis_size("sub")
    cont, nodes = initial_voltage.shape[1:]
    ports = initial_history.shape[2]
    capacity = max(2, 2 * ports // n_subs)
    slots = n_subs * capacity
    start = initial_history[0]
    opens = open_step[0]
    delay = line_delay
    impedance = surge_impedance
    port_shape = ((cont, ports), F32)
    split_shape = ((PARTS, cont, nodes), F32)

    inputs = [source_amp, source_phase, companion, initial_voltage[0], start, delay, opens, partner_sub]
    table, target, order, high, low, partial = call(
        lambda *refs: first_body(capacity, len(inputs), *refs),
        [
            ((2 * STEPS, nodes), F32),
            ((1, ports), jnp.int32),
            ((nodes, nodes), BF16),
            ((PARTS, nodes, nodes), BF16),
            ((PARTS, nodes, nodes), BF16),
            split_shape,
        ],
        away=[*inputs, matrix],
        scratch=[
            *[pltpu.VMEM(array.shape, array.dtype) for array in inputs],
            pltpu.SemaphoreType.DMA((len(inputs),)),
            pltpu.VMEM((STRIDE, PARTS * nodes, ports), F32),
            pltpu.SemaphoreType.DMA((PARTS, STRIDE)),
        ],
        name="first_step",
    )

    history = start
    far = []
    for step in range(STEPS):
        anchors = [a for a in range(step) if DMIN <= step - a <= DMAX]
        if step % 2 == 1:
            partial, history, *before = call(
                lambda *refs, step=step, anchors=anchors: odd_body(step, anchors, *refs),
                [split_shape, port_shape] + [port_shape] * (step + DMIN < STEPS),
                high,
                low,
                table,
                start,
                delay,
                opens,
                impedance,
                history,
                arrived,
                *[far[a] for a in anchors],
                name=f"step_{step}",
            )
        elif step > 0:
            anchors = anchors[:-1]
            partial, history, *newest = call(
                lambda *refs, step=step, anchors=anchors: even_body(step, anchors, *refs),
                [split_shape] + [port_shape] * 3,
                high,
                low,
                table,
                start,
                delay,
                opens,
                target,
                volt,
                incoming.reshape(slots, 2 * cont),
                *[far[a] for a in anchors],
                name=f"step_{step}",
            )
            far += newest
        arrived = lax.all_to_all(partial, "split", split_axis=0, concat_axis=0, tiled=True)
        if step == STEPS - 1:
            volt, current = call(
                lambda *refs, step=step: last_body(step, *refs),
                [((cont, nodes), F32), port_shape],
                arrived,
                impedance,
                history,
                opens,
                order,
                name="last",
            )
        elif step % 2 == 1:
            volt, buffer = call(
                lambda *refs, step=step: route_body(step, *refs),
                [((cont, nodes), F32), ((slots, 2 * cont), F32)],
                arrived,
                impedance,
                history,
                opens,
                target,
                *before,
                name=f"route_{step}",
            )
            buffer = buffer.reshape(n_subs, capacity, 2 * cont)
            incoming = lax.all_to_all(buffer, "sub", split_axis=0, concat_axis=0, tiled=True)
    return (volt[None], current[None])


def solution(mesh):
    placed = (
        P("sub", None, "split"),
        P("sub", "split"),
        P("sub", "split"),
        P("sub", "split"),
        P("sub", "split"),
        P("sub", None, "split"),
        P("sub", None, "split"),
        P("sub", "split"),
        P("sub", "split"),
        P("sub", None, "split"),
    )
    return jax.shard_map(
        local,
        mesh=mesh,
        in_specs=placed,
        out_specs=(P("sub", None, "split"), P("sub", None, "split")),
        check_vma=False,
    )
```

```python
import jax
import jax.numpy as jnp
from jax import lax
from jax.experimental import pallas as pl
from jax.experimental.pallas import tpu as pltpu
from jax.sharding import PartitionSpec as P

STEPS = 8
DMIN = 2
DMAX = 5
STRIDE = 4
PARTS = 4

angular = 0.7

F32 = jnp.float32
BF16 = jnp.bfloat16
NT = (((1,), (1,)), ((), ()))
NN = (((1,), (0,)), ((), ()))
TN = (((0,), (0,)), ((), ()))


def two_pieces(array):
    high = array.astype(BF16)
    return high, (array - high.astype(F32)).astype(BF16)


def exact_dot(array, onehot, dims, array_first=True):
    high = array.astype(BF16)
    rest = array - high.astype(F32)
    middle = rest.astype(BF16)
    low = (rest - middle.astype(F32)).astype(BF16)
    total = None
    for piece in (high, middle, low):
        pair = (piece, onehot) if array_first else (onehot, piece)
        term = lax.dot_general(*pair, dims, preferred_element_type=F32)
        total = term if total is None else total + term
    return total


def stacked_exact_dot(array, onehot, dims):
    rows = array.shape[0]
    high = array.astype(BF16)
    rest = array - high.astype(F32)
    middle = rest.astype(BF16)
    low = (rest - middle.astype(F32)).astype(BF16)
    pieces = jnp.concatenate([high, middle, low], 0)
    terms = lax.dot_general(pieces, onehot, dims, preferred_element_type=F32)
    return terms[:rows] + terms[rows : 2 * rows] + terms[2 * rows :]


def iota(shape, dim):
    return lax.broadcasted_iota(jnp.int32, shape, dim)


def start_strips(matrix, strips, sems):
    copies = []
    width = strips.shape[2]
    for strip in range(strips.shape[0]):
        columns = matrix.at[:, pl.ds(strip * width, width)]
        copies.append(pltpu.make_async_copy(columns, strips.at[strip], sems.at[strip]))
        copies[-1].start()
    return copies


def strip_rows(strips, part, strip):
    nodes = strips.shape[1] // PARTS
    ports = nodes // STRIDE
    pieces = [strips[strip, pl.ds(part * nodes + lane, ports, stride=STRIDE), :] for lane in range(STRIDE)]
    return jnp.concatenate(pieces, 0)


def port_first(size):
    node = iota((1, size), 1)
    new = (node % STRIDE) * (size // STRIDE) + node // STRIDE
    return (iota((size, size), 0) == new).astype(F32).astype(BF16)


def product(stacked, cont, high, low, dims):
    both = lax.dot_general(stacked, high, dims, preferred_element_type=F32)
    rest = lax.dot_general(stacked[:cont], low, dims, preferred_element_type=F32)
    return both[:cont] + both[cont:] + rest


def first_body(capacity, count, *refs):
    ins, refs = refs[: count + 1], refs[count + 1 :]
    matrix = ins[-1]
    table, target, order, high, low, out, *held = refs
    *held, small_sems, strips, sems = held
    fetches = [pltpu.make_async_copy(a, b, small_sems.at[n]) for n, (a, b) in enumerate(zip(ins, held))]
    copies = start_strips(matrix, strips, sems)
    for copy in fetches:
        copy.start()
    cont, nodes = held[3].shape
    ports = nodes // STRIDE
    moved = port_first(nodes)
    order[...] = moved
    width = 2 * ports
    moved = port_first(width)
    chunk = width // STRIDE
    for copy in fetches:
        copy.wait()
    amp, phase, comp, volt, start, delay, opens, partner = held
    times = (iota((STEPS, nodes), 0) + 1).astype(F32)
    source = amp[...] * jnp.cos(angular * times + phase[...])
    given = jnp.concatenate([volt[...], source, jnp.broadcast_to(comp[...], (STEPS, nodes))], 0)
    given = stacked_exact_dot(given, order[...], NT)
    table[...] = given[cont:]
    across = jnp.broadcast_to(partner[...].astype(F32), (ports, ports))
    earlier = (across == across.T) & (iota((ports, ports), 0) < iota((ports, ports), 1))
    rank = jnp.sum(earlier.astype(F32), axis=0, keepdims=True).astype(jnp.int32)
    target[...] = partner[...] * capacity + rank
    history = history_at(0, start[...], delay[...], [])
    stacked = stacked_right(0, given[:cont], history, table, opens)
    for copy in copies:
        copy.wait()
    for part in range(PARTS):
        for pair in range(nodes // width):
            rows = jnp.concatenate([strip_rows(strips, part, strip) for strip in (2 * pair, 2 * pair + 1)], 1)
            for piece, piece_out in zip(two_pieces(rows), (high, low)):
                term = lax.dot_general(moved, piece, NT, preferred_element_type=F32).astype(BF16)
                for lane in range(STRIDE):
                    here = lane * ports + pair * chunk
                    piece_out[part, here : here + chunk, :] = term[lane * chunk : (lane + 1) * chunk]
        if part > 0:
            out[part - 1] = product(stacked, cont, high[part - 1], low[part - 1], NN)
    out[PARTS - 1] = product(stacked, cont, high[PARTS - 1], low[PARTS - 1], NN)


def history_at(step, start, delay, far):
    history = jnp.where(step < delay, start, 0.0)
    for anchor, array in far:
        history = jnp.where(delay == step - anchor, -array, history)
    return history


def total_of(partial):
    total = partial[0]
    for part in range(1, PARTS):
        total = total + partial[part]
    return total


def outgoing_of(step, total, impedance, history, opens):
    ports = impedance.shape[1]
    value = 2.0 * total[:, :ports] / impedance[...] + history
    return jnp.where(step < opens[...], value, 0.0)


def onehot_of(target, slots):
    return (iota((slots, target.shape[1]), 0) == target[...]).astype(F32).astype(BF16)


def stacked_right(step, volt, history, table, opens):
    ports = history.shape[1]
    right = table[step : step + 1] + table[STEPS : STEPS + 1] * volt
    inject = jnp.where(step < opens[...], history, 0.0)
    right = jnp.concatenate([right[:, :ports] - inject, right[:, ports:]], 1)
    return jnp.concatenate(two_pieces(right), 0)


def multiply(step, volt, history, high, low, table, opens, out):
    stacked = stacked_right(step, volt, history, table, opens)
    cont = volt.shape[0]
    rest = [jnp.dot(stacked[:cont], low[part], preferred_element_type=F32) for part in range(PARTS)]
    for part in range(PARTS):
        both = jnp.dot(stacked, high[part], preferred_element_type=F32)
        out[part] = both[:cont] + both[cont:] + rest[part]


def odd_body(step, anchors, high, low, table, start, delay, opens, impedance, history, partial, *refs):
    far = [(anchor, ref[...]) for anchor, ref in zip(anchors, refs)]
    out, kept, *outgoing = refs[len(anchors) :]
    total = total_of(partial)
    for ref in outgoing:
        ref[...] = outgoing_of(step - 1, total, impedance, history[...], opens)
    now = history_at(step, start[...], delay[...], far)
    kept[...] = now
    multiply(step, total, now, high, low, table, opens, out)


def even_body(step, anchors, high, low, table, start, delay, opens, target, volt, buffer, *refs):
    out, kept, *newest = refs[len(anchors) :]
    cont, nodes = volt.shape
    half = nodes // 2
    right = table[step : step + 1] + table[STEPS : STEPS + 1] * volt[...]
    stacked = jnp.concatenate(two_pieces(right[:, half:]), 0)
    for part in range(PARTS):
        out[part] = product(stacked, cont, high[part, half:], low[part, half:], NN)
    ports = start.shape[1]
    both = exact_dot(buffer[...], onehot_of(target, buffer.shape[0]), TN)
    latest = [both[:cont], both[cont:]]
    for ref, array in zip(newest, latest):
        ref[...] = array
    far = [(anchor, ref[...]) for anchor, ref in zip(anchors, refs)] + [(step - DMIN, latest[0])]
    now = history_at(step, start[...], delay[...], far)
    kept[...] = now
    inject = jnp.where(step < opens[...], now, 0.0)
    lower = jnp.concatenate([right[:, :ports] - inject, right[:, ports:half]], 1)
    stacked = jnp.concatenate(two_pieces(lower), 0)
    for part in range(PARTS):
        out[part] += product(stacked, cont, high[part, :half], low[part, :half], NN)


def route_body(step, partial, impedance, history, opens, target, before, volt, buffer):
    total = total_of(partial)
    volt[...] = total
    outgoing = outgoing_of(step, total, impedance, history[...], opens)
    both = jnp.concatenate([before[...], outgoing], 0)
    buffer[...] = exact_dot(both, onehot_of(target, buffer.shape[0]), NT, array_first=False)


def last_body(step, partial, impedance, history, opens, order, volt, current):
    total = total_of(partial)
    ports = impedance.shape[1]
    value = total[:, :ports] / impedance[...] + history[...]
    current[...] = jnp.where(step < opens[...], value, 0.0)
    volt[...] = stacked_exact_dot(total, order[...], NN)


def call(body, shapes, *arrays, name, away=(), scratch=()):
    whole = pl.BlockSpec(memory_space=pltpu.VMEM)
    return pl.pallas_call(
        body,
        in_specs=[whole] * len(arrays) + [pl.BlockSpec(memory_space=pltpu.HBM)] * len(away),
        out_specs=[whole] * len(shapes),
        out_shape=[jax.ShapeDtypeStruct(shape, kind) for shape, kind in shapes],
        scratch_shapes=list(scratch),
        compiler_params=pltpu.CompilerParams(vmem_limit_bytes=40 << 20),
        name=name,
    )(*arrays, *[pltpu.with_memory_space_constraint(array, pltpu.HBM) for array in away])


def local(
    inv_conductance,
    source_amp,
    source_phase,
    companion,
    surge_impedance,
    initial_voltage,
    initial_history,
    partner_sub,
    line_delay,
    open_step,
):
    matrix = inv_conductance[0]
    n_subs = lax.axis_size("sub")
    cont, nodes = initial_voltage.shape[1:]
    ports = initial_history.shape[2]
    capacity = max(2, 2 * ports // n_subs)
    slots = n_subs * capacity
    start = initial_history[0]
    opens = open_step[0]
    delay = line_delay
    impedance = surge_impedance
    port_shape = ((cont, ports), F32)
    split_shape = ((PARTS, cont, nodes), F32)

    inputs = [source_amp, source_phase, companion, initial_voltage[0], start, delay, opens, partner_sub]
    table, target, order, high, low, partial = call(
        lambda *refs: first_body(capacity, len(inputs), *refs),
        [
            ((2 * STEPS, nodes), F32),
            ((1, ports), jnp.int32),
            ((nodes, nodes), BF16),
            ((PARTS, nodes, nodes), BF16),
            ((PARTS, nodes, nodes), BF16),
            split_shape,
        ],
        away=[*inputs, matrix],
        scratch=[
            *[pltpu.VMEM(array.shape, array.dtype) for array in inputs],
            pltpu.SemaphoreType.DMA((len(inputs),)),
            pltpu.VMEM((STRIDE, PARTS * nodes, ports), F32),
            pltpu.SemaphoreType.DMA((STRIDE,)),
        ],
        name="first_step",
    )

    history = start
    far = []
    for step in range(STEPS):
        anchors = [a for a in range(step) if DMIN <= step - a <= DMAX]
        if step % 2 == 1:
            partial, history, *before = call(
                lambda *refs, step=step, anchors=anchors: odd_body(step, anchors, *refs),
                [split_shape, port_shape] + [port_shape] * (step + DMIN < STEPS),
                high,
                low,
                table,
                start,
                delay,
                opens,
                impedance,
                history,
                arrived,
                *[far[a] for a in anchors],
                name=f"step_{step}",
            )
        elif step > 0:
            anchors = anchors[:-1]
            partial, history, *newest = call(
                lambda *refs, step=step, anchors=anchors: even_body(step, anchors, *refs),
                [split_shape] + [port_shape] * 3,
                high,
                low,
                table,
                start,
                delay,
                opens,
                target,
                volt,
                incoming.reshape(slots, 2 * cont),
                *[far[a] for a in anchors],
                name=f"step_{step}",
            )
            far += newest
        arrived = lax.all_to_all(partial, "split", split_axis=0, concat_axis=0, tiled=True)
        if step == STEPS - 1:
            volt, current = call(
                lambda *refs, step=step: last_body(step, *refs),
                [((cont, nodes), F32), port_shape],
                arrived,
                impedance,
                history,
                opens,
                order,
                name="last",
            )
        elif step % 2 == 1:
            volt, buffer = call(
                lambda *refs, step=step: route_body(step, *refs),
                [((cont, nodes), F32), ((slots, 2 * cont), F32)],
                arrived,
                impedance,
                history,
                opens,
                target,
                *before,
                name=f"route_{step}",
            )
            buffer = buffer.reshape(n_subs, capacity, 2 * cont)
            incoming = lax.all_to_all(buffer, "sub", split_axis=0, concat_axis=0, tiled=True)
    return (volt[None], current[None])


def solution(mesh):
    placed = (
        P("sub", None, "split"),
        P("sub", "split"),
        P("sub", "split"),
        P("sub", "split"),
        P("sub", "split"),
        P("sub", None, "split"),
        P("sub", None, "split"),
        P("sub", "split"),
        P("sub", "split"),
        P("sub", None, "split"),
    )
    return jax.shard_map(
        local,
        mesh=mesh,
        in_specs=placed,
        out_specs=(P("sub", None, "split"), P("sub", None, "split")),
        check_vma=False,
    )
```
